32 devices in a mesh: grp: 2 (over y), ctx: 4 (over z), head: 2 (over x), rep: 2 (over core).
Axes of the slice: x: 2, y: 2, z: 4, core: 2. Of those that a mesh axis runs over, the one named last changes fastest.
Arguments:
- queries: bfloat16 [8192, 2048], P(('grp', 'ctx', 'head', 'rep')), parts along dimension 0, may hold values from -10 to 10
- keys: bfloat16 [8192, 2048], P(('grp', 'ctx', 'head', 'rep')), parts along dimension 0, may hold values from -10 to 10
- values: bfloat16 [8192, 2048], P(('grp', 'ctx', 'head', 'rep')), parts along dimension 0, may hold values from -6 to 6
- reads: int32 [16, 8], P('grp'), parts along dimension 0, may hold values from 0 to 1, as said below
- owner: int32 [16], P('grp'), parts along dimension 0, may hold values from 0 to 7, as said below
Outputs:
- attended: bfloat16 [8192, 2048], P(('grp', 'ctx', 'head', 'rep')), parts along dimension 0
The draws below stay inside these ranges and needn't reach their ends.
There are 2 independent parts, one for each index of `grp`. The reference program is written for one: setup_inputs(seed, part) draws one part's arguments, and reference() takes and returns one part's arrays. A program takes and returns all parts, laid end to end along the dimension named above; each array names one. Nothing has to cross between parts.
Inputs may be any that keep to these rules, and one draw needn't show every extreme that they name: `owner`: A permutation of the blocks in which sequence block b sits in slot b or in slot b with its lowest bit flipped. Every block reads itself; reads[kb, qb] is nonzero only where |kb - qb| <= 2 and |owner[kb] - owner[qb]| <= 3.
All inputs are finite; a program needn't handle non-finite values.
Results may differ from the reference program's by a relative error of at most 0.0047.
Values may be sent and summed in bfloat16 or wider, within the bound.
No kernel may reach another device: no remote copies, remote signals or barrier semaphores. Data moves between devices by JAX's collectives and lax.ppermute only.
A program may use at most 64 MiB of HBM per device.

```python
import math
import jax
import jax.numpy as jnp
from jax import lax

HEADS = 32
HEAD_DIM = 64
BLOCK = 512
REACH = 3
NBLK = 8
TOKENS = 4096
HD = 2048


def block_layout(key):
    pair_key, level_key, near_key = jax.random.split(jax.random.fold_in(key, 11), 3)
    blocks = jnp.arange(NBLK, dtype=jnp.int32)
    pair_ids = jnp.arange(NBLK // 2, dtype=jnp.int32)
    flips = jax.random.randint(pair_key, (NBLK // 2,), 0, 2, dtype=jnp.int32)
    centre = NBLK // 4 * 2
    centre_pair = centre // 2
    if NBLK >= 8:
        flips = jnp.where(pair_ids == 1, 1, flips)
        flips = jnp.where((pair_ids == 3) | (pair_ids == 4), 0, flips)
        flips = jnp.where(pair_ids == centre_pair, 1, flips)
        flips = jnp.where(pair_ids == centre_pair + 1, 0, flips)
    owner = blocks ^ jnp.repeat(flips, 2)
    levels = jax.random.randint(level_key, (NBLK,), 1, 6, dtype=jnp.int32)
    tosses = jax.random.randint(near_key, (NBLK, NBLK), 0, 8, dtype=jnp.int32)
    key_grid = blocks[:, None]
    query_grid = blocks[None, :]
    apart = jnp.abs(key_grid - query_grid)
    near = (apart >= 1) & (apart <= 2) & (tosses < levels[None, :])
    forced = (key_grid == 1) & (query_grid == 2) | (key_grid == 2) & (query_grid == 1)
    forced = forced | (key_grid == 4) & (query_grid == 5) | (key_grid == 5) & (query_grid == 4)
    forced = forced | (key_grid == 6) & (query_grid == 8) | (key_grid == 8) & (query_grid == 6)
    if NBLK >= 8:
        middle_reader = query_grid == centre + 1
        middle_keys = (key_grid == centre - 1) | (key_grid == centre) | (key_grid == centre + 2) | (key_grid == centre + 3)
        forced = forced | middle_reader & middle_keys
        forced = forced | (query_grid == centre) & ((key_grid == centre - 2) | (key_grid == centre - 1))
    reads = ((apart == 0) | near | forced).astype(jnp.int32)
    return (owner, reads)


def draw_owner(key, part):
    return block_layout(key)[0]


def draw_reads(key, part):
    return block_layout(key)[1]


def draw_queries(key, part):
    base = jnp.clip(jax.random.normal(jax.random.fold_in(key, 1), (TOKENS, HEADS * HEAD_DIM), jnp.float32), -6.0, 6.0)
    return base.astype(jnp.bfloat16)


def draw_keys(key, part):
    base = jnp.clip(jax.random.normal(jax.random.fold_in(key, 2), (TOKENS, HEADS * HEAD_DIM), jnp.float32), -6.0, 6.0)
    return base.astype(jnp.bfloat16)


def shard_levels(key, dims, pieces, smallest, top_value):
    def one(axis_at, blocks):
        heights = jax.random.uniform(jax.random.fold_in(jax.random.fold_in(key, 6), axis_at), (blocks,), jnp.float32, smallest / len(pieces), top_value / len(pieces))
        return jnp.repeat(jnp.exp(heights), dims[axis_at] // blocks).reshape((-1,) + (1,) * (len(dims) - axis_at - 1))

    loudness = one(*pieces[0])
    for cut in pieces[1:]:
        loudness = loudness * one(*cut)
    return loudness


def centred(rng, extent, width, limit, cuts=(), kind=jnp.bfloat16):
    values = width * jax.random.normal(rng, extent, jnp.float32)
    if cuts:
        values = values * shard_levels(rng, extent, cuts, -0.22, 0.18)
    return jnp.clip(values, -limit, limit).astype(kind)


def setup_inputs(seed: int = 0, part: int = 0) -> dict:
    streams_of = jax.random.split(jax.random.key(seed), 6)
    part_splits = jax.random.split(jax.random.fold_in(streams_of[5], part), 6)
    return {
        "queries": draw_queries(jax.random.fold_in(jax.random.fold_in(streams_of[5], part), 71), part),
        "keys": draw_keys(jax.random.fold_in(jax.random.fold_in(streams_of[5], part), 71), part),
        "values": centred(part_splits[2], (TOKENS, HD), 1.0, 6.0, ((0, 16),)),
        "reads": draw_reads(jax.random.fold_in(jax.random.fold_in(streams_of[5], part), 71), part),
        "owner": draw_owner(jax.random.fold_in(jax.random.fold_in(streams_of[5], part), 71), part),
    }


def reference(queries, keys, values, reads, owner):
    highest = lax.Precision.HIGHEST
    block_count = TOKENS // BLOCK
    slots = jnp.arange(block_count, dtype=jnp.int32)
    placed = (owner[:, None] == slots[None, :]).astype(jnp.float32)
    slot_reads = jnp.dot(jnp.dot(placed.T, reads.astype(jnp.float32), precision=highest), placed, precision=highest)
    padded_reads = jnp.pad(slot_reads, ((REACH, REACH), (0, 0)))
    window_len = 2 * REACH + 1
    scale_factor = 1.0 / math.sqrt(HEAD_DIM)

    def blocked(array):
        shaped = array.astype(jnp.float32).reshape(block_count, BLOCK, HEADS, HEAD_DIM)
        return jnp.pad(shaped, ((REACH, REACH), (0, 0), (0, 0), (0, 0)))
    key_pad = blocked(keys)
    value_pad = blocked(values)

    def one_block(query_slot):
        column = lax.dynamic_index_in_dim(padded_reads, query_slot, 1, keepdims=False)
        allowed = lax.dynamic_slice_in_dim(column, query_slot, window_len) > 0.5
        key_mask = jnp.repeat(allowed, BLOCK)
        query_block = lax.dynamic_slice_in_dim(queries, query_slot * BLOCK, BLOCK, 0).astype(jnp.float32)
        query_block = query_block.reshape(BLOCK, HEADS, HEAD_DIM).transpose(1, 0, 2)
        key_window = lax.dynamic_slice_in_dim(key_pad, query_slot, window_len, 0).reshape(window_len * BLOCK, HEADS, HEAD_DIM).transpose(1, 0, 2)
        value_window = lax.dynamic_slice_in_dim(value_pad, query_slot, window_len, 0).reshape(window_len * BLOCK, HEADS, HEAD_DIM).transpose(1, 0, 2)

        def one_head(operands):
            query_rows, key_rows, value_rows = operands
            scores = jnp.dot(query_rows, key_rows.T, precision=highest) * scale_factor
            scores = jnp.where(key_mask[None, :], scores, -jnp.inf)
            row_max = lax.optimization_barrier(jnp.max(scores, axis=1, keepdims=True))
            weights = jnp.exp(scores - row_max)
            row_total = lax.optimization_barrier(jnp.sum(weights, axis=1, keepdims=True))
            rounded = lax.optimization_barrier(weights.astype(jnp.bfloat16)).astype(jnp.float32)
            return jnp.dot(rounded, value_rows, precision=highest) / row_total
        per_head = lax.map(one_head, (query_block, key_window, value_window))
        return per_head.transpose(1, 0, 2).reshape(BLOCK, HEADS * HEAD_DIM).astype(jnp.bfloat16)
    blocks_out = lax.map(one_block, slots)
    return blocks_out.reshape(TOKENS, HEADS * HEAD_DIM)
```

```python
import functools

import jax
import jax.numpy as jnp
from jax import lax
from jax.experimental import pallas as pl
from jax.experimental.pallas import tpu as pltpu
from jax.sharding import PartitionSpec as P

HEAD_DIM = 64
BLOCK = 512
LANES = 128


VMEM = pl.BlockSpec(memory_space=pltpu.VMEM)
SMEM = pl.BlockSpec(memory_space=pltpu.SMEM)
ANY = pl.BlockSpec(memory_space=pl.ANY)


def exchange_peer(x, j):
    size = lax.axis_size("head") * lax.axis_size("rep")
    return lax.ppermute(x, ("head", "rep"), [(i, i ^ j) for i in range(size)])


def exchange_ctx(x, parity):
    ctxs, reps = lax.axis_size("ctx"), lax.axis_size("rep")
    pairs = []
    for i in range(ctxs):
        other = i + 1 if i % 2 == parity else i - 1
        for r in range(reps):
            if 0 <= other < ctxs:
                pairs.append((i * reps + r, other * reps + r))
            elif reps % 2 == 0:
                pairs.append((i * reps + r, i * reps + (r ^ 1)))
    return lax.ppermute(x, ("ctx", "rep"), pairs)


def pack_body(dims, reads_ref, owner_ref, q_ref, k_ref, v_ref, *rest):
    peers, chunks, rows, blk_dev, span = dims
    plan_ref, kv_refs, q_refs = rest[0], rest[1 : 1 + peers * chunks], rest[1 + peers * chunks : -1]
    sem = rest[-1]
    me = lax.axis_index("head") * lax.axis_size("rep") + lax.axis_index("rep")
    copies = []
    for c in range(chunks):
        for j in range(peers):
            start = pl.multiple_of((me ^ j) * (chunks * LANES) + c * LANES, LANES)
            cols = pl.ds(start, LANES)
            kv, q = kv_refs[c * peers + j], q_refs[c * peers + j]
            for src, dst in ((k_ref, kv.at[0]), (v_ref, kv.at[1]), (q_ref, q)):
                copies.append(pltpu.make_async_copy(src.at[:, cols], dst, sem))
    for copy in copies:
        copy.start()
    ctx = lax.axis_index("ctx")
    blocks = owner_ref.shape[0]
    odd = ctx % 2
    around = (ctx + 1 - 2 * odd, ctx, ctx - 1 + 2 * odd)
    first = (me * rows) // BLOCK

    def block_of(slot):
        return jnp.where(owner_ref[slot] == slot, slot, slot ^ 1)

    for t in range(blk_dev):
        query = block_of(ctx * blk_dev + (first ^ t))
        count = jnp.int32(0)
        for source in range(3):
            where = around[source]
            inside = jnp.logical_and(where >= 0, where < blocks // blk_dev)
            safe = jnp.where(inside, where, ctx)
            for s in range(blk_dev):
                key = block_of(safe * blk_dev + (first ^ s))
                used = jnp.logical_and(inside, reads_ref[key, query] > 0)
                plan_ref[t * span + 1 + count] = source * blk_dev + s
                count = count + used.astype(jnp.int32)
        plan_ref[t * span] = count
    for copy in copies:
        copy.wait()


def attend_body(dims, plan_ref, *rest):
    peers, rows, blk_dev, span = dims
    q_refs, kv_refs, o_refs = rest[:peers], rest[peers : 4 * peers], rest[4 * peers : 5 * peers]
    k_all, v_all, s_all = rest[5 * peers :]
    per_block = BLOCK // rows
    lower = lax.broadcasted_iota(jnp.int32, (rows, LANES), 1) < HEAD_DIM
    for source in range(3):
        for j in range(peers):
            kv = kv_refs[source * peers + j]
            b, at = source * blk_dev + j // per_block, pl.ds((j % per_block) * rows, rows)
            k_all[b, at, :] = kv[0]
            v = kv[1]
            one = jnp.ones_like(v)
            v_all[0, b, at, :] = jnp.where(lower, v, one)
            v_all[1, b, at, :] = jnp.where(lower, one, v)
    first_half = lax.broadcasted_iota(jnp.int32, (BLOCK, LANES), 1) < HEAD_DIM
    for t in range(blk_dev):
        q = jnp.concatenate([q_refs[t * per_block + i][...] for i in range(per_block)], axis=0)
        q = q * jnp.bfloat16(1.0 / HEAD_DIM**0.5)
        zero = jnp.zeros_like(q)
        q_heads = (jnp.where(first_half, q, zero), jnp.where(first_half, zero, q))
        count = plan_ref[t * span]

        def score(i, largest):
            b = plan_ref[t * span + 1 + i]
            k = k_all[b]
            new = []
            for h in range(2):
                s = lax.dot_general(q_heads[h], k, (((1,), (1,)), ((), ())), preferred_element_type=jnp.float32)
                s_all[h, i] = s
                m = s[:, :LANES]
                for at in range(LANES, BLOCK, LANES):
                    m = jnp.maximum(m, s[:, at : at + LANES])
                new.append(jnp.maximum(largest[h], m))
            return tuple(new)

        lowest = jnp.full((BLOCK, LANES), -jnp.inf, jnp.float32)
        largest = lax.fori_loop(0, count, score, (lowest, lowest))
        row_max = tuple(jnp.max(m, axis=1, keepdims=True) for m in largest)

        def weigh(i, sums):
            b = plan_ref[t * span + 1 + i]
            new = []
            for h in range(2):
                p = jnp.exp(s_all[h, i] - row_max[h]).astype(jnp.bfloat16)
                new.append(sums[h] + jnp.dot(p, v_all[h, b], preferred_element_type=jnp.float32))
            return tuple(new)

        zeros = jnp.zeros((BLOCK, LANES), jnp.float32)
        even, odd = lax.fori_loop(0, count, weigh, (zeros, zeros))
        total = pltpu.roll(jnp.where(first_half, odd, even), HEAD_DIM, 1)
        out = (jnp.where(first_half, even, odd) / total).astype(jnp.bfloat16)
        for i in range(per_block):
            o_refs[t * per_block + i][...] = out[i * rows : (i + 1) * rows]


def unpack_body(dims, *refs):
    peers, chunks = dims
    out_ref, sem = refs[-2], refs[-1]
    me = lax.axis_index("head") * lax.axis_size("rep") + lax.axis_index("rep")
    copies = []
    for c in range(chunks):
        for j in range(peers):
            start = pl.multiple_of((me ^ j) * (chunks * LANES) + c * LANES, LANES)
            copies.append(pltpu.make_async_copy(refs[c * peers + j], out_ref.at[:, pl.ds(start, LANES)], sem))
    for copy in copies:
        copy.start()
    for copy in copies:
        copy.wait()


def shards(queries, keys, values, reads, owner):
    rows, feats = queries.shape
    peers = lax.axis_size("head") * lax.axis_size("rep")
    chunks = feats // peers // LANES
    blk_dev = rows * peers // BLOCK
    assert blk_dev % 2 == 0 and BLOCK % rows == 0 and peers & (peers - 1) == 0
    span = 3 * blk_dev + 2
    bf16 = jnp.bfloat16
    piece = jax.ShapeDtypeStruct((rows, LANES), bf16)
    packed = pl.pallas_call(
        functools.partial(pack_body, (peers, chunks, rows, blk_dev, span)),
        out_shape=[jax.ShapeDtypeStruct((blk_dev * span,), jnp.int32)]
        + [jax.ShapeDtypeStruct((2, rows, LANES), bf16)] * (peers * chunks)
        + [piece] * (peers * chunks),
        in_specs=[SMEM, SMEM, ANY, ANY, ANY],
        out_specs=[SMEM] + [VMEM] * (2 * peers * chunks),
        scratch_shapes=[pltpu.SemaphoreType.DMA],
        name="pack",
    )(reads, owner, queries, keys, values)
    plan, kv_sent, q_sent = packed[0], packed[1 : 1 + peers * chunks], packed[1 + peers * chunks :]
    attend = pl.pallas_call(
        functools.partial(attend_body, (peers, rows, blk_dev, span)),
        out_shape=[piece] * peers,
        in_specs=[SMEM] + [VMEM] * (4 * peers),
        out_specs=[VMEM] * peers,
        scratch_shapes=[
            pltpu.VMEM((3 * blk_dev, BLOCK, LANES), bf16),
            pltpu.VMEM((2, 3 * blk_dev, BLOCK, LANES), bf16),
            pltpu.VMEM((2, 3 * blk_dev, BLOCK, BLOCK), jnp.float32),
        ],
        compiler_params=pltpu.CompilerParams(vmem_limit_bytes=32 << 20),
        cost_estimate=pl.CostEstimate(flops=8 * 10**9, bytes_accessed=4 << 20, transcendentals=6 * 10**6),
        name="attend",
    )
    results = []
    for c in range(chunks):
        kv_own = [kv_sent[c * peers]] + [exchange_peer(kv_sent[c * peers + j], j) for j in range(1, peers)]
        q_own = [q_sent[c * peers]] + [exchange_peer(q_sent[c * peers + j], j) for j in range(1, peers)]
        edges = [[exchange_ctx(kv, parity) for kv in kv_own] for parity in (0, 1)]
        out = attend(plan, *q_own, *edges[0], *kv_own, *edges[1])
        results += [out[0]] + [exchange_peer(out[j], j) for j in range(1, peers)]
    return pl.pallas_call(
        functools.partial(unpack_body, (peers, chunks)),
        out_shape=jax.ShapeDtypeStruct((rows, feats), bf16),
        in_specs=[VMEM] * (peers * chunks),
        out_specs=ANY,
        scratch_shapes=[pltpu.SemaphoreType.DMA],
        name="unpack",
    )(*results)


def solution(mesh):
    placed = (
        P(("grp", "ctx", "head", "rep"), None),
        P(("grp", "ctx", "head", "rep"), None),
        P(("grp", "ctx", "head", "rep"), None),
        P("grp", None),
        P("grp"),
    )
    return jax.shard_map(
        shards,
        mesh=mesh,
        in_specs=placed,
        out_specs=P(("grp", "ctx", "head", "rep"), None),
        check_vma=False,
    )
```

```python
import functools

import jax
import jax.numpy as jnp
from jax import lax
from jax.experimental import pallas as pl
from jax.experimental.pallas import tpu as pltpu
from jax.sharding import PartitionSpec as P

HEAD_DIM = 64
BLOCK = 512
LANES = 128


VMEM = pl.BlockSpec(memory_space=pltpu.VMEM)
SMEM = pl.BlockSpec(memory_space=pltpu.SMEM)
ANY = pl.BlockSpec(memory_space=pl.ANY)


def exchange_peer(x, j):
    size = lax.axis_size("head") * lax.axis_size("rep")
    return lax.ppermute(x, ("head", "rep"), [(i, i ^ j) for i in range(size)])


def exchange_ctx(x, parity):
    ctxs, reps = lax.axis_size("ctx"), lax.axis_size("rep")
    pairs = []
    for i in range(ctxs):
        other = i + 1 if i % 2 == parity else i - 1
        for r in range(reps):
            if 0 <= other < ctxs:
                pairs.append((i * reps + r, other * reps + r))
            elif reps % 2 == 0:
                pairs.append((i * reps + r, i * reps + (r ^ 1)))
    return lax.ppermute(x, ("ctx", "rep"), pairs)


def own_index():
    return lax.axis_index("head") * lax.axis_size("rep") + lax.axis_index("rep")


def pack_body(chunks, peers, parts, *refs):
    arrays, outs, sem = refs[:3], refs[-1 - peers : -1], refs[-1]
    me = own_index()
    copies = []
    for j, out in enumerate(outs):
        for i, (array, c) in enumerate(parts):
            start = pl.multiple_of((me ^ j) * (chunks * LANES) + c * LANES, LANES)
            copies.append(pltpu.make_async_copy(arrays[array].at[:, pl.ds(start, LANES)], out.at[i], sem))
    for copy in copies:
        copy.start()
    for copy in copies:
        copy.wait()


def plan_body(rows, blk_dev, span, reads_ref, owner_ref, plan_ref):
    ctx = lax.axis_index("ctx")
    blocks = owner_ref.shape[0]
    odd = ctx % 2
    around = (ctx + 1 - 2 * odd, ctx, ctx - 1 + 2 * odd)
    first = (own_index() * rows) // BLOCK

    def block_of(slot):
        return jnp.where(owner_ref[slot] == slot, slot, slot ^ 1)

    for t in range(blk_dev):
        query = block_of(ctx * blk_dev + (first ^ t))
        count = jnp.int32(0)
        for source in range(3):
            where = around[source]
            inside = jnp.logical_and(where >= 0, where < blocks // blk_dev)
            safe = jnp.where(inside, where, ctx)
            for s in range(blk_dev):
                key = block_of(safe * blk_dev + (first ^ s))
                used = jnp.logical_and(inside, reads_ref[key, query] > 0)
                plan_ref[t * span + 1 + count] = source * blk_dev + s
                count = count + used.astype(jnp.int32)
        plan_ref[t * span] = count


def merge_body(peers, rows, *refs):
    out = refs[-1]
    for j in range(peers):
        last = refs[j].shape[0]
        out[0, j * rows : (j + 1) * rows, :] = refs[j][last - 2]
        out[1, j * rows : (j + 1) * rows, :] = refs[j][last - 1]


def attend_body(dims, plan_ref, *rest):
    peers, rows, blk_dev, span, q_at, before = dims
    q_refs, kv_refs, rest = rest[:peers], rest[peers : peers + 3], rest[peers + 3 :]
    before_refs, rest = rest[: before * peers], rest[before * peers :]
    o_refs, (k_all, v_all, s_all) = rest[-3 - peers : -3], rest[-3:]
    per_block = BLOCK // rows
    lower = lax.broadcasted_iota(jnp.int32, (BLOCK, LANES), 1) < HEAD_DIM
    for i in range(before):
        for j in range(peers):
            o_refs[j][i] = before_refs[i * peers + j][0]
    for source in range(3):
        for s in range(blk_dev):
            b, at = source * blk_dev + s, pl.ds(s * BLOCK, BLOCK)
            k_all[b] = kv_refs[source][0, at, :]
            v = kv_refs[source][1, at, :]
            one = jnp.ones_like(v)
            v_all[0, b] = jnp.where(lower, v, one)
            v_all[1, b] = jnp.where(lower, one, v)
    for t in range(blk_dev):
        q = jnp.concatenate([q_refs[t * per_block + i][q_at] for i in range(per_block)], axis=0)
        q = q * jnp.bfloat16(1.0 / HEAD_DIM**0.5)
        zero = jnp.zeros_like(q)
        q_heads = (jnp.where(lower, q, zero), jnp.where(lower, zero, q))
        count = plan_ref[t * span]

        def score(i, largest):
            b = plan_ref[t * span + 1 + i]
            k = k_all[b]
            new = []
            for h in range(2):
                s = lax.dot_general(q_heads[h], k, (((1,), (1,)), ((), ())), preferred_element_type=jnp.float32)
                s_all[h, i] = s
                m = s[:, :LANES]
                for at in range(LANES, BLOCK, LANES):
                    m = jnp.maximum(m, s[:, at : at + LANES])
                new.append(jnp.maximum(largest[h], m))
            return tuple(new)

        lowest = jnp.full((BLOCK, LANES), -jnp.inf, jnp.float32)
        largest = lax.fori_loop(0, count, score, (lowest, lowest))
        row_max = tuple(jnp.max(m, axis=1, keepdims=True) for m in largest)

        def weigh(i, sums):
            b = plan_ref[t * span + 1 + i]
            new = []
            for h in range(2):
                p = jnp.exp(s_all[h, i] - row_max[h]).astype(jnp.bfloat16)
                new.append(sums[h] + jnp.dot(p, v_all[h, b], preferred_element_type=jnp.float32))
            return tuple(new)

        zeros = jnp.zeros((BLOCK, LANES), jnp.float32)
        even, odd = lax.fori_loop(0, count, weigh, (zeros, zeros))
        total = pltpu.roll(jnp.where(lower, odd, even), HEAD_DIM, 1)
        out = (jnp.where(lower, even, odd) / total).astype(jnp.bfloat16)
        for i in range(per_block):
            o_refs[t * per_block + i][before] = out[i * rows : (i + 1) * rows]


def unpack_body(chunks, first, pieces, *refs):
    out_ref, sem = refs[-2], refs[-1]
    me = own_index()
    copies = []
    for j, piece in enumerate(refs[:pieces]):
        for i in range(piece.shape[0]):
            start = pl.multiple_of((me ^ j) * (chunks * LANES) + (first + i) * LANES, LANES)
            copies.append(pltpu.make_async_copy(piece.at[i], out_ref.at[:, pl.ds(start, LANES)], sem))
    for copy in copies:
        copy.start()
    for copy in copies:
        copy.wait()


def shards(queries, keys, values, reads, owner):
    rows, feats = queries.shape
    peers = lax.axis_size("head") * lax.axis_size("rep")
    chunks = feats // peers // LANES
    blk_dev = rows * peers // BLOCK
    assert blk_dev % 2 == 0 and BLOCK % rows == 0 and peers & (peers - 1) == 0 and chunks >= 2
    span = 3 * blk_dev + 2
    bf16 = jnp.bfloat16
    tile = rows * LANES * 2

    def buffer(n):
        return jax.ShapeDtypeStruct((n, rows, LANES), bf16)

    def params(n):
        return pltpu.CompilerParams(vmem_limit_bytes=n << 20)

    plan = pl.pallas_call(
        functools.partial(plan_body, rows, blk_dev, span),
        out_shape=jax.ShapeDtypeStruct((blk_dev * span,), jnp.int32),
        in_specs=[SMEM, SMEM],
        out_specs=SMEM,
        compiler_params=params(2),
        name="plan",
    )(reads, owner)

    def pack(c, after):
        parts = [(0, c - 1)] * (c > 0) + [(0, c)] * (c == chunks - 1) + [(1, c), (2, c)]
        moved = 2 * peers * len(parts) * tile
        return pl.pallas_call(
            functools.partial(pack_body, chunks, peers, parts),
            out_shape=[buffer(len(parts))] * peers,
            in_specs=[ANY] * (3 + len(after)),
            out_specs=[VMEM] * peers,
            scratch_shapes=[pltpu.SemaphoreType.DMA],
            compiler_params=params(2),
            cost_estimate=pl.CostEstimate(flops=0, bytes_accessed=moved, transcendentals=0),
            name="pack",
        )(queries, keys, values, *after)

    def merge(c, pieces, after):
        return pl.pallas_call(
            functools.partial(merge_body, peers, rows),
            out_shape=jax.ShapeDtypeStruct((2, peers * rows, LANES), bf16),
            in_specs=[VMEM] * peers + [ANY] * len(after),
            out_specs=VMEM,
            compiler_params=params(2),
            cost_estimate=pl.CostEstimate(flops=0, bytes_accessed=4 * peers * tile, transcendentals=0),
            name="merge",
        )(*pieces, *after)

    def attend(q_at, q_pieces, kv, before, after):
        n = len(before) + 1
        return pl.pallas_call(
            functools.partial(attend_body, (peers, rows, blk_dev, span, q_at, n - 1)),
            out_shape=[buffer(n)] * peers,
            in_specs=[SMEM] + [VMEM] * (peers + 3 + (n - 1) * peers) + [ANY] * len(after),
            out_specs=[VMEM] * peers,
            scratch_shapes=[
                pltpu.VMEM((3 * blk_dev, BLOCK, LANES), bf16),
                pltpu.VMEM((2, 3 * blk_dev, BLOCK, LANES), bf16),
                pltpu.VMEM((2, 3 * blk_dev, BLOCK, BLOCK), jnp.float32),
            ],
            compiler_params=params(24),
            cost_estimate=pl.CostEstimate(flops=8 * 10**9, bytes_accessed=4 << 20, transcendentals=6 * 10**6),
            name="attend",
        )(plan, *q_pieces, *kv, *[piece for old in before for piece in old], *after)

    def swap(pieces):
        return [pieces[0]] + [exchange_peer(pieces[j], j) for j in range(1, peers)]

    sent, packs = [], []
    for c in range(chunks):
        packs.append(pack(c, packs[-1][:1] if packs else []))
        sent.append(swap(packs[-1]))

    merged, edges, outs = {}, {}, []

    def shift(c, after):
        merged[c] = merge(c, sent[c], after)
        edges[c] = [exchange_ctx(merged[c], parity) for parity in (0, 1)]

    shift(0, [packs[-1][0]])
    shift(1, [merged[0]])
    for c in range(chunks):
        group, q_at = (sent[c + 1], 0) if c < chunks - 1 else (sent[c], 1)
        before = outs if c == chunks - 2 else []
        after = [merged[min(c + 1, chunks - 1)]] + [old[0] for old in outs[-1:]]
        outs.append(attend(q_at, group, (edges[c][0], merged[c], edges[c][1]), before, after))
        if c + 2 < chunks:
            shift(c + 2, [outs[-1][0]])
    early, late = swap(outs[-2]), swap(outs[-1])

    def unpack(first, pieces, into):
        return pl.pallas_call(
            functools.partial(unpack_body, chunks, first, peers),
            out_shape=jax.ShapeDtypeStruct((rows, feats), bf16),
            in_specs=[VMEM] * peers + [ANY] * len(into),
            out_specs=ANY,
            scratch_shapes=[pltpu.SemaphoreType.DMA],
            input_output_aliases={peers: 0} if into else {},
            compiler_params=params(2),
            cost_estimate=pl.CostEstimate(flops=0, bytes_accessed=2 * peers * tile * pieces[0].shape[0], transcendentals=0),
            name="unpack",
        )(*pieces, *into)

    return unpack(chunks - 1, late, [unpack(0, early, [])])


def solution(mesh):
    placed = (
        P(("grp", "ctx", "head", "rep"), None),
        P(("grp", "ctx", "head", "rep"), None),
        P(("grp", "ctx", "head", "rep"), None),
        P("grp", None),
        P("grp"),
    )
    return jax.shard_map(
        shards,
        mesh=mesh,
        in_specs=placed,
        out_specs=P(("grp", "ctx", "head", "rep"), None),
        check_vma=False,
    )
```

```python
import functools

import jax
import jax.numpy as jnp
from jax import lax
from jax.experimental import pallas as pl
from jax.experimental.pallas import tpu as pltpu
from jax.sharding import PartitionSpec as P

HEAD_DIM = 64
BLOCK = 512
LANES = 128
ONES = 16


VMEM = pl.BlockSpec(memory_space=pltpu.VMEM)
SMEM = pl.BlockSpec(memory_space=pltpu.SMEM)
ANY = pl.BlockSpec(memory_space=pl.ANY)
HBM = pl.BlockSpec(memory_space=pltpu.HBM)


def exchange_peer(x, j):
    size = lax.axis_size("head") * lax.axis_size("rep")
    return lax.ppermute(x, ("head", "rep"), [(i, i ^ j) for i in range(size)])


def exchange_ctx(x, parity):
    ctxs, reps = lax.axis_size("ctx"), lax.axis_size("rep")
    pairs = []
    for i in range(ctxs):
        other = i + 1 if i % 2 == parity else i - 1
        for r in range(reps):
            if 0 <= other < ctxs:
                pairs.append((i * reps + r, other * reps + r))
            elif reps % 2 == 0:
                pairs.append((i * reps + r, i * reps + (r ^ 1)))
    return lax.ppermute(x, ("ctx", "rep"), pairs)


def own_index():
    return lax.axis_index("head") * lax.axis_size("rep") + lax.axis_index("rep")


def pack_body(chunks, sends, *refs):
    arrays, outs, sem = refs[:3], refs[-1 - len(sends) : -1], refs[-1]
    me = own_index()
    copies = []
    for out, (j, parts) in zip(outs, sends):
        for i, (array, c) in enumerate(parts):
            start = pl.multiple_of((me ^ j) * (chunks * LANES) + c * LANES, LANES)
            copies.append(pltpu.make_async_copy(arrays[array].at[:, pl.ds(start, LANES)], out.at[i], sem))
    for copy in copies:
        copy.start()
    for copy in copies:
        copy.wait()


def plan_body(rows, blk_dev, span, reads_ref, owner_ref, plan_ref):
    ctx = lax.axis_index("ctx")
    blocks = owner_ref.shape[0]
    odd = ctx % 2
    around = (ctx + 1 - 2 * odd, ctx, ctx - 1 + 2 * odd)
    first = (own_index() * rows) // BLOCK

    def block_of(slot):
        return jnp.where(owner_ref[slot] == slot, slot, slot ^ 1)

    for t in range(blk_dev):
        query = block_of(ctx * blk_dev + (first ^ t))
        count = jnp.int32(0)
        for source in range(3):
            where = around[source]
            inside = jnp.logical_and(where >= 0, where < blocks // blk_dev)
            safe = jnp.where(inside, where, ctx)
            for s in range(blk_dev):
                key = block_of(safe * blk_dev + (first ^ s))
                used = jnp.logical_and(inside, reads_ref[key, query] > 0)
                plan_ref[t * span + 1 + count] = source * blk_dev + s
                count = count + used.astype(jnp.int32)
        plan_ref[t * span] = count


def merge_body(others, rows, *refs):
    out = refs[-1]
    for i in range(others):
        last = refs[i].shape[0]
        out[0, i * rows : (i + 1) * rows, :] = refs[i][last - 2]
        out[1, i * rows : (i + 1) * rows, :] = refs[i][last - 1]


def attend_body(dims, plan_ref, *rest):
    peers, rows, blk_dev, span, chunk, q_at, before, unroll = dims
    q_own, q_refs, rest = rest[0], rest[1:peers], rest[peers:]
    own_refs, other_refs, rest = rest[:3], rest[3:6], rest[6:]
    before_refs, rest = rest[: before * peers], rest[before * peers :]
    o_refs, (k_all, v_all, q_all, sums, *halves) = rest[-8 - peers : -8], rest[-8:]
    scores, tops = halves[:2], halves[2:]
    per_block = BLOCK // rows
    lower = lax.broadcasted_iota(jnp.int32, (BLOCK, LANES), 1) < HEAD_DIM
    for i in range(before):
        for j in range(peers):
            o_refs[j][i] = before_refs[i * peers + j][0]

    def tokens(source, which, s):
        other = other_refs[source][which, max(s * BLOCK - rows, 0) : (s + 1) * BLOCK - rows, :]
        return other if s else jnp.concatenate([own_refs[source][2 * chunk + which], other], axis=0)

    for source in range(3):
        for s in range(blk_dev):
            b = source * blk_dev + s
            k_all[b] = tokens(source, 0, s)
            flipped = tokens(source, 1, s).T
            for h in range(2):
                v_all[b, h, :HEAD_DIM] = flipped[h * HEAD_DIM : (h + 1) * HEAD_DIM]
                v_all[b, h, HEAD_DIM:] = jnp.ones((ONES, BLOCK), jnp.bfloat16)
    for t in range(blk_dev):
        pieces = [q_refs[j - 1][q_at] if j else q_own[chunk] for j in range(t * per_block, (t + 1) * per_block)]
        q = jnp.concatenate(pieces, axis=0) * jnp.bfloat16(1.0 / HEAD_DIM**0.5)
        zero = jnp.zeros_like(q)
        q_all[2 * t] = jnp.where(lower, q, zero)
        q_all[2 * t + 1] = jnp.where(lower, zero, q)

    def score(u, i):
        b = plan_ref[u // 2 * span + 1 + i]
        s = lax.dot_general(k_all[b], q_all[u], (((1,), (1,)), ((), ())), preferred_element_type=jnp.float32)
        scores[u % 2][i] = s
        top = tops[u % 2]
        top[...] = jnp.maximum(top[...], jnp.max(s.reshape(BLOCK // 8, 8, BLOCK), axis=0))

    def weigh(u, i):
        b = plan_ref[u // 2 * span + 1 + i]
        p = jnp.exp(scores[u % 2][i] - tops[u % 2][0:1, :]).astype(jnp.bfloat16)
        sums[u] += jnp.dot(v_all[b, u % 2], p, preferred_element_type=jnp.float32)

    def loop(start, stop, step, by):
        def one(i, carry):
            step(i)
            return carry

        def several(i, carry):
            for x in range(by):
                step(start + i * by + x)
            return carry

        times = (stop - start) // by if by > 1 else 0
        if by > 1:
            lax.fori_loop(0, times, several, 0)
        lax.fori_loop(start + times * by, stop, one, 0)

    units = 2 * blk_dev
    counts = [plan_ref[t * span] for t in range(blk_dev)]
    for k in range(units + 1):
        if k < units:
            tops[k % 2][...] = jnp.full((8, BLOCK), -jnp.inf, jnp.float32)

        def both(i, k=k):
            score(k, i)
            weigh(k - 1, i)

        if k == 0:
            loop(0, counts[0], functools.partial(score, 0), unroll)
        elif k == units:
            loop(0, counts[-1], functools.partial(weigh, k - 1), unroll)
        elif k % 2:
            loop(0, counts[k // 2], both, unroll)
        else:
            weighed, scored = counts[k // 2 - 1], counts[k // 2]
            shared = jnp.minimum(weighed, scored)
            loop(0, shared, both, unroll)
            loop(shared, weighed, functools.partial(weigh, k - 1), 1)
            loop(shared, scored, functools.partial(score, k), 1)
        if k < units:
            top = tops[k % 2]
            top[...] = jnp.broadcast_to(jnp.max(top[...], axis=0, keepdims=True), (8, BLOCK))
            sums[k] = jnp.zeros((HEAD_DIM + ONES, BLOCK), jnp.float32)
    for t in range(blk_dev):
        heads = [sums[2 * t + h, :HEAD_DIM] / sums[2 * t + h, HEAD_DIM : HEAD_DIM + 1] for h in range(2)]
        out = jnp.concatenate(heads, axis=0).T.astype(jnp.bfloat16)
        for i in range(per_block):
            o_refs[t * per_block + i][before] = out[i * rows : (i + 1) * rows]


def unpack_body(chunks, first, pieces, *refs):
    out_ref, sem = refs[-2], refs[-1]
    me = own_index()
    copies = []
    for j, piece in enumerate(refs[:pieces]):
        for i in range(piece.shape[0]):
            start = pl.multiple_of((me ^ j) * (chunks * LANES) + (first + i) * LANES, LANES)
            copies.append(pltpu.make_async_copy(piece.at[i], out_ref.at[:, pl.ds(start, LANES)], sem))
    for copy in copies:
        copy.start()
    for copy in copies:
        copy.wait()


def shards(queries, keys, values, reads, owner):
    rows, feats = queries.shape
    peers = lax.axis_size("head") * lax.axis_size("rep")
    chunks = feats // peers // LANES
    blk_dev = rows * peers // BLOCK
    assert blk_dev % 2 == 0 and BLOCK % rows == 0 and peers & (peers - 1) == 0 and chunks >= 2
    span = 3 * blk_dev + 2
    bf16 = jnp.bfloat16
    queries, keys, values = (pltpu.with_memory_space_constraint(x, pltpu.HBM) for x in (queries, keys, values))
    tile = rows * LANES * 2

    def buffer(n):
        return jax.ShapeDtypeStruct((n, rows, LANES), bf16)

    def params(n):
        return pltpu.CompilerParams(vmem_limit_bytes=n << 20)

    plan = pl.pallas_call(
        functools.partial(plan_body, rows, blk_dev, span),
        out_shape=jax.ShapeDtypeStruct((blk_dev * span,), jnp.int32),
        in_specs=[SMEM, SMEM],
        out_specs=SMEM,
        compiler_params=params(2),
        name="plan",
    )(reads, owner)

    def pack(sends, after):
        moved = 2 * tile * sum(len(parts) for _, parts in sends)
        return pl.pallas_call(
            functools.partial(pack_body, chunks, sends),
            out_shape=[buffer(len(parts)) for _, parts in sends],
            in_specs=[HBM] * 3 + [ANY] * len(after),
            out_specs=[VMEM] * len(sends),
            scratch_shapes=[pltpu.SemaphoreType.DMA],
            compiler_params=params(2),
            cost_estimate=pl.CostEstimate(flops=0, bytes_accessed=moved, transcendentals=0),
            name="pack",
        )(queries, keys, values, *after)

    def merge(pieces, after):
        return pl.pallas_call(
            functools.partial(merge_body, peers - 1, rows),
            out_shape=jax.ShapeDtypeStruct((2, (peers - 1) * rows, LANES), bf16),
            in_specs=[VMEM] * (peers - 1) + [ANY] * len(after),
            out_specs=VMEM,
            compiler_params=params(2),
            cost_estimate=pl.CostEstimate(flops=0, bytes_accessed=4 * peers * tile, transcendentals=0),
            name="merge",
        )(*pieces, *after)

    def attend(c, q_at, queries_in, sources, before, after):
        n = len(before) + 1
        f32 = jnp.float32
        return pl.pallas_call(
            functools.partial(attend_body, (peers, rows, blk_dev, span, c, q_at, n - 1, 2)),
            out_shape=[buffer(n)] * peers,
            in_specs=[SMEM] + [VMEM] * (peers + 6 + (n - 1) * peers) + [ANY] * len(after),
            out_specs=[VMEM] * peers,
            scratch_shapes=[
                pltpu.VMEM((3 * blk_dev, BLOCK, LANES), bf16),
                pltpu.VMEM((3 * blk_dev, 2, HEAD_DIM + ONES, BLOCK), bf16),
                pltpu.VMEM((2 * blk_dev, BLOCK, LANES), bf16),
                pltpu.VMEM((2 * blk_dev, HEAD_DIM + ONES, BLOCK), f32),
                *[pltpu.VMEM((3 * blk_dev, BLOCK, BLOCK), f32)] * 2,
                *[pltpu.VMEM((8, BLOCK), f32)] * 2,
            ],
            compiler_params=params(24),
            cost_estimate=pl.CostEstimate(flops=8 * 10**9, bytes_accessed=4 << 20, transcendentals=6 * 10**6),
            name="attend",
        )(plan, *queries_in, *sources, *[piece for old in before for piece in old], *after)

    def swap(pieces):
        return [pieces[0]] + [exchange_peer(pieces[j], j) for j in range(1, peers)]

    def parts(c):
        return [(0, c - 1)] * (c > 0) + [(0, c)] * (c == chunks - 1 and c > 0) + [(1, c), (2, c)]

    others = range(1, peers)
    own_parts = [(1 + i % 2, i // 2) for i in range(2 * chunks)]
    own, *first = pack([(0, own_parts)] + [(j, parts(0)) for j in others], [])
    own_edges = [exchange_ctx(own, parity) for parity in (0, 1)]
    sent = [[exchange_peer(x, j) for j, x in zip(others, first)]]
    q_own, *rest = pack([(0, [(0, c) for c in range(chunks)])] + [(j, parts(c)) for c in range(1, chunks) for j in others], [own])
    for c in range(1, chunks):
        group = rest[(c - 1) * (peers - 1) : c * (peers - 1)]
        sent.append([exchange_peer(x, j) for j, x in zip(others, group)])

    merged, edges, outs = {}, {}, []

    def shift(c, after):
        merged[c] = merge(sent[c], after)
        edges[c] = [exchange_ctx(merged[c], parity) for parity in (0, 1)]

    shift(0, [q_own])
    shift(1, [merged[0]])
    for c in range(chunks):
        group, q_at = (sent[c + 1], 0) if c < chunks - 1 else (sent[c], 1)
        before = outs if c == chunks - 2 else []
        after = [merged[min(c + 1, chunks - 1)]] + [old[0] for old in outs[-1:]]
        sources = (own_edges[0], own, own_edges[1], edges[c][0], merged[c], edges[c][1])
        outs.append(attend(c, q_at, [q_own, *group], sources, before, after))
        if c + 2 < chunks:
            shift(c + 2, [outs[-1][0]])
    early, late = swap(outs[-2]), swap(outs[-1])

    def unpack(first, pieces, into):
        return pl.pallas_call(
            functools.partial(unpack_body, chunks, first, peers),
            out_shape=jax.ShapeDtypeStruct((rows, feats), bf16),
            in_specs=[VMEM] * peers + [ANY] * len(into),
            out_specs=ANY,
            scratch_shapes=[pltpu.SemaphoreType.DMA],
            input_output_aliases={peers: 0} if into else {},
            compiler_params=params(2),
            cost_estimate=pl.CostEstimate(flops=0, bytes_accessed=2 * peers * tile * pieces[0].shape[0], transcendentals=0),
            name="unpack",
        )(*pieces, *into)

    return unpack(chunks - 1, late, [unpack(0, early, [])])


def solution(mesh):
    placed = (
        P(("grp", "ctx", "head", "rep"), None),
        P(("grp", "ctx", "head", "rep"), None),
        P(("grp", "ctx", "head", "rep"), None),
        P("grp", None),
        P("grp"),
    )
    return jax.shard_map(
        shards,
        mesh=mesh,
        in_specs=placed,
        out_specs=P(("grp", "ctx", "head", "rep"), None),
        check_vma=False,
    )
```
